32 devices in a mesh: groups: 2 (over x), tm: 8 (over z, y), tensor: 2 (over core).
Axes of the slice: x: 2, y: 2, z: 4, core: 2. Of those that a mesh axis runs over, the one named last changes fastest.
Arguments:
- frames_in: bfloat16 [4096, 6144], P(('groups', 'tm', 'tensor')), parts along dimension 0, may hold values from -6 to 6
- cotangent: bfloat16 [4096, 6144], P(('groups', 'tm', 'tensor')), parts along dimension 0, may hold values from -6 to 6
- down_weight: bfloat16 [6144, 384], P('tensor'), may hold values from -0.078125 to 0.078125
- down_bias: float32 [384], replicated, may hold values from -4 to 4
- conv_kernel: float32 [3, 384], replicated, may hold values from -3 to 3
- up_weight: bfloat16 [6144, 384], P('tensor'), may hold values from -0.3125 to 0.3125
- up_bias: float32 [6144], replicated, may hold values from -3 to 3
- ln_gain: float32 [6144], replicated, may hold values from 0.5 to 1.5
Outputs:
- out_tokens: bfloat16 [4096, 6144], P(('groups', 'tm', 'tensor')), parts along dimension 0
- grad_down: float32 [12288, 384], P(('groups', 'tm', 'tensor')), parts along dimension 0
- grad_up: float32 [12288, 384], P(('groups', 'tm', 'tensor')), parts along dimension 0
- grad_up_bias: float32 [12288], P(('groups', 'tm', 'tensor')), parts along dimension 0
- grad_down_bias: float32 [768], P('groups'), parts along dimension 0
- grad_kernel: float32 [6, 384], P('groups'), parts along dimension 0
The draws below stay inside these ranges and needn't reach their ends.
There are 2 independent parts, one for each index of `groups`. The reference program is written for one: setup_inputs(seed, part) draws one part's arguments, and reference() takes and returns one part's arrays. A program takes and returns all parts, laid end to end along the dimension named above; an argument that names none is the same for every part. Nothing has to cross between parts.
All inputs are finite; a program needn't handle non-finite values.
Results may differ from the reference program's by a relative error of at most 0.0085.
Values may be sent and summed in bfloat16 or wider, within the bound.
No kernel may reach another device: no remote copies, remote signals or barrier semaphores. Data moves between devices by JAX's collectives and lax.ppermute only.
A program may use at most 128 MiB of HBM per device.

```python
import jax
import jax.numpy as jnp
from jax import lax

D = 6144
RA = 384
FRAMES = 8
SPATIAL = 256
TOKENS = 2048


def with_spikes(array, key, source, target, shards_of, factor):
    owner, partner = [(jnp.arange(array.shape[dim]) // (array.shape[dim] // shards_of)).reshape([-1 if axis == dim else 1 for axis in range(array.ndim)]) for dim in (source, target)]
    chosen = jax.random.permutation(key, shards_of)[partner]
    strong = (owner == chosen) | (owner == (partner + shards_of // 2) % shards_of)
    return jnp.where(strong, factor * array, array)


def block_scale(own_key, shape, shards, smallest, largest):
    loudness, own = 1.0, jax.random.fold_in(own_key, 6)
    for position, parts in shards:
        draws = jnp.exp(jax.random.uniform(jax.random.fold_in(own, position), (parts,), jnp.float32, smallest / len(shards), largest / len(shards)))
        loudness = loudness * jnp.repeat(draws, shape[position] // parts).reshape([-1 if axis == position else 1 for axis in range(len(shape))])
    return loudness


def noise(stream_key, extent, scale, reach, pieces=(), held_as=jnp.bfloat16):
    result = scale * jax.random.normal(stream_key, extent, jnp.float32)
    if pieces:
        result = result * block_scale(stream_key, extent, pieces, -0.22, 0.18)
    return jnp.clip(result, -reach, reach).astype(held_as)


def noise_with(own_key, extent, scale, reach, pieces, heavy, dtype=jnp.bfloat16):
    array = scale * jax.random.normal(own_key, extent, jnp.float32)
    if pieces:
        array = array * block_scale(own_key, extent, pieces, -0.22, 0.18)
    return jnp.clip(with_spikes(array, jax.random.fold_in(own_key, 3), *heavy), -reach, reach).astype(dtype)


def setup_inputs(seed: int = 0, part: int = 0) -> dict:
    keys = jax.random.split(jax.random.key(seed), 9)
    own_keys = jax.random.split(jax.random.fold_in(keys[8], part), 9)
    frames_in = noise_with(own_keys[0], (TOKENS, D), 1.0, 6.0, ((0, 16),), (0, 1, 16, 2.0))
    cotangent = noise_with(own_keys[1], (TOKENS, D), 1.0, 6.0, ((0, 16),), (0, 1, 16, 2.0))
    down_weight = noise(keys[2], (D, RA), D ** -0.5, 0.078125, ((0, 2),))
    down_bias = noise(keys[3], (RA,), 1.0, 4.0, (), jnp.float32)
    conv_kernel = noise(keys[4], (3, RA), 0.6, 3.0, (), jnp.float32)
    up_weight = noise(keys[5], (D, RA), RA ** -0.5, 0.3125, ((0, 2),))
    up_bias = noise(keys[6], (D,), 0.5, 3.0, (), jnp.float32)
    ln_gain = jnp.clip(1.0 + 0.1 * jax.random.normal(keys[7], (D,), jnp.float32), 0.5, 1.5)
    return {"frames_in": frames_in, "cotangent": cotangent, "down_weight": down_weight, "down_bias": down_bias, "conv_kernel": conv_kernel, "up_weight": up_weight, "up_bias": up_bias, "ln_gain": ln_gain}


epsilon = 1e-06

def frame_earlier(stack):
    blank = jnp.zeros_like(stack[:1])
    return jnp.concatenate([blank, stack[:-1]], axis=0)

def frame_later(stack):
    blank = jnp.zeros_like(stack[:1])
    return jnp.concatenate([stack[1:], blank], axis=0)

def temporal_forward(stack, kernel):
    return kernel[0] * frame_earlier(stack) + kernel[1] * stack + kernel[2] * frame_later(stack)

def temporal_backward(stack, kernel):
    return kernel[0] * frame_later(stack) + kernel[1] * stack + kernel[2] * frame_earlier(stack)

def norm_forward(lifted, ln_gain):
    lifted_wide = lifted.astype(jnp.float32)
    center = lax.optimization_barrier(jnp.mean(lifted_wide, axis=-1, keepdims=True))
    shifted = lifted_wide - center
    spread = lax.optimization_barrier(jnp.mean(shifted * shifted, axis=-1, keepdims=True))
    inverse = lax.rsqrt(spread + epsilon)
    unit = shifted * inverse
    return (unit, inverse, (unit * ln_gain).astype(jnp.bfloat16))

def norm_backward(grad_normed, unit, inverse, ln_gain):
    scaled = grad_normed * ln_gain
    return inverse * (scaled - lax.optimization_barrier(jnp.mean(scaled, axis=-1, keepdims=True)) - unit * lax.optimization_barrier(jnp.mean(scaled * unit, axis=-1, keepdims=True)))

def inner_rows(left, right):
    return lax.dot_general(left, right, (((0,), (0,)), ((), ())), preferred_element_type=jnp.float32)

def reference(frames_in, cotangent, down_weight, down_bias, conv_kernel, up_weight, up_bias, ln_gain):
    bottle = (jnp.dot(frames_in, down_weight, preferred_element_type=jnp.float32) + down_bias).astype(jnp.bfloat16)
    bottle_stack = bottle.astype(jnp.float32).reshape(FRAMES, SPATIAL, RA)
    conv = temporal_forward(bottle_stack, conv_kernel).reshape(TOKENS, RA).astype(jnp.bfloat16)
    raised = lax.dot_general(conv, up_weight, (((1,), (1,)), ((), ())), preferred_element_type=jnp.float32)
    lifted = (frames_in.astype(jnp.float32) + raised + up_bias).astype(jnp.bfloat16)
    unit, inverse, out_tokens = norm_forward(lifted, ln_gain)
    grad_lifted = norm_backward(cotangent.astype(jnp.float32), unit, inverse, ln_gain).astype(jnp.bfloat16)
    grad_conv = jnp.dot(grad_lifted, up_weight, preferred_element_type=jnp.float32).astype(jnp.bfloat16)
    conv_stack = grad_conv.astype(jnp.float32).reshape(FRAMES, SPATIAL, RA)
    grad_bottle = temporal_backward(conv_stack, conv_kernel).reshape(TOKENS, RA).astype(jnp.bfloat16)
    grad_up = inner_rows(grad_lifted, conv)
    grad_up_bias = lax.optimization_barrier(jnp.sum(grad_lifted.astype(jnp.float32), axis=0))
    grad_down = inner_rows(frames_in, grad_bottle)
    grad_down_bias = lax.optimization_barrier(jnp.sum(grad_bottle.astype(jnp.float32), axis=0))
    grad_kernel = jnp.stack([lax.optimization_barrier(jnp.sum(frame_earlier(bottle_stack) * conv_stack, axis=(0, 1))), lax.optimization_barrier(jnp.sum(bottle_stack * conv_stack, axis=(0, 1))), lax.optimization_barrier(jnp.sum(frame_later(bottle_stack) * conv_stack, axis=(0, 1)))], axis=0)
    return (out_tokens, grad_down, grad_up, grad_up_bias, grad_down_bias, grad_kernel)
```

```python
import jax
import jax.numpy as jnp
from jax import lax
from jax.sharding import PartitionSpec as P

epsilon = 1e-06
cores = 2
block_frames = 4
narrow, wide = jnp.bfloat16, jnp.float32


def norm_forward(lifted, ln_gain):
    lifted_wide = lifted.astype(wide)
    center = jnp.mean(lifted_wide, axis=-1, keepdims=True)
    shifted = lifted_wide - center
    spread = jnp.mean(shifted * shifted, axis=-1, keepdims=True)
    inverse = lax.rsqrt(spread + epsilon)
    unit = shifted * inverse
    return (unit, inverse, (unit * ln_gain).astype(narrow))


def norm_backward(grad_normed, unit, inverse, ln_gain):
    scaled = grad_normed * ln_gain
    return inverse * (
        scaled
        - jnp.mean(scaled, axis=-1, keepdims=True)
        - unit * jnp.mean(scaled * unit, axis=-1, keepdims=True)
    )


def inner_rows(left, right):
    return lax.dot_general(
        left, right, (((0,), (0,)), ((), ())), preferred_element_type=wide
    )


def outer_rows(left, right):
    return lax.dot_general(
        left, right, (((1,), (1,)), ((), ())), preferred_element_type=wide
    )


def high_low(values):
    high = values.astype(narrow)
    return jnp.concatenate([high, (values - high.astype(wide)).astype(narrow)], axis=0)


def local(frames_in, cotangent, down_weight, down_bias, conv_kernel, up_weight, up_bias, ln_gain):
    tokens, features = frames_in.shape
    channels = down_weight.shape[1]
    count = lax.axis_size("tm")
    blocks = count // block_frames
    share = features // (count * cores)
    frame, core = lax.axis_index("tm"), lax.axis_index("tensor")
    block, place = frame // block_frames, frame % block_frames

    def core_swap(value):
        return lax.ppermute(value, "tensor", [(0, 1), (1, 0)])

    def block_swap(value, step):
        return lax.ppermute(value, "tm", [(i, i ^ step) for i in range(count)])

    def neighbours(value):
        earlier = lax.ppermute(value, "tm", [(i, i + 1) for i in range(count - 1)])
        later = lax.ppermute(value, "tm", [(i + 1, i) for i in range(count - 1)])
        return earlier, later

    def columns_for(value, step):
        return [
            lax.dynamic_slice_in_dim(
                value,
                ((piece * block_frames + (place ^ step)) * cores) * share,
                cores * share,
                axis=1,
            )
            for piece in range(blocks)
        ]

    def exchange(value):
        parts = [jnp.concatenate(columns_for(value, step), axis=0) for step in range(block_frames)]
        parts = [parts[0]] + [block_swap(parts[step], step) for step in range(1, block_frames)]
        kept = [lax.dynamic_slice_in_dim(p, core * share, share, axis=1) for p in parts]
        sent = [lax.dynamic_slice_in_dim(p, (1 - core) * share, share, axis=1) for p in parts]
        got = core_swap(jnp.concatenate(sent, axis=0))
        kept = jnp.concatenate(kept, axis=0)
        return [v.reshape(block_frames, blocks, tokens, share) for v in (kept, got)]

    def gather(value):
        rows = value.shape[0]
        own = jnp.concatenate(
            [value] + [block_swap(value, step) for step in range(1, block_frames)], axis=0
        )
        return [v.reshape(block_frames, rows, -1) for v in (own, core_swap(own))]

    def contract(pairs, rows, piece):
        total = 0.0
        for features_of, row in zip(pairs, rows):
            chosen = lax.dynamic_index_in_dim(features_of, piece, axis=1, keepdims=False)
            total = total + inner_rows(chosen.reshape(-1, share), row.reshape(-1, channels))
        return total

    down_other = core_swap(down_weight)
    half = features // cores
    bottle = (
        jnp.dot(
            lax.dynamic_slice_in_dim(frames_in, core * half, half, axis=1),
            down_weight,
            preferred_element_type=wide,
        )
        + jnp.dot(
            lax.dynamic_slice_in_dim(frames_in, (1 - core) * half, half, axis=1),
            down_other,
            preferred_element_type=wide,
        )
        + down_bias
    ).astype(narrow)
    up_other = core_swap(up_weight)
    up_full = jnp.where(
        core == 0,
        jnp.concatenate([up_weight, up_other], axis=0),
        jnp.concatenate([up_other, up_weight], axis=0),
    )
    frames_share = exchange(frames_in)
    before, after = [v.astype(wide) for v in neighbours(bottle)]
    here = bottle.astype(wide)
    conv = (conv_kernel[0] * before + conv_kernel[1] * here + conv_kernel[2] * after).astype(narrow)
    conv_rows = gather(conv)
    lifted = (frames_in.astype(wide) + outer_rows(conv, up_full) + up_bias).astype(narrow)
    unit, inverse, out_tokens = norm_forward(lifted, ln_gain)
    grad_lifted = norm_backward(cotangent.astype(wide), unit, inverse, ln_gain).astype(narrow)
    grad_conv = jnp.dot(grad_lifted, up_full, preferred_element_type=wide).astype(narrow)
    own_grad = grad_conv.astype(wide)
    grad_before, grad_after = [v.astype(wide) for v in neighbours(grad_conv)]
    grad_bottle = (
        conv_kernel[0] * grad_after + conv_kernel[1] * own_grad + conv_kernel[2] * grad_before
    ).astype(narrow)
    small = jnp.stack(
        [
            jnp.sum(before * own_grad, axis=0),
            jnp.sum(here * own_grad, axis=0),
            jnp.sum(after * own_grad, axis=0),
            jnp.sum(grad_bottle.astype(wide), axis=0),
        ],
        axis=0,
    )
    pad = jnp.zeros((8, channels), narrow)
    bottle_rows = gather(jnp.concatenate([grad_bottle, high_low(small), pad], axis=0))
    small_rows = [v[:, tokens:] for v in bottle_rows]
    bottle_rows = [v[:, :tokens] for v in bottle_rows]
    small = sum(
        jnp.sum(v[:, :4].astype(wide), axis=0) + jnp.sum(v[:, 4:8].astype(wide), axis=0)
        for v in small_rows
    )
    grad_share = exchange(grad_lifted)

    def bias_of(piece):
        total = 0.0
        for value in grad_share:
            chosen = lax.dynamic_index_in_dim(value, piece, axis=1, keepdims=False)
            total = total + jnp.sum(chosen.astype(wide), axis=(0, 1))
        return total

    def across(value, step):
        return lax.ppermute(
            value,
            "tm",
            [(i, (i + step * block_frames) % count) for i in range(count)],
        )

    grad_down = contract(frames_share, bottle_rows, block)
    grad_up = contract(grad_share, conv_rows, block)
    grad_up_bias = bias_of(block)
    own_small = small
    for step in range(1, blocks):
        target = (block + step) % blocks
        down_got = across(
            jnp.concatenate(
                [
                    contract(frames_share, bottle_rows, target).astype(narrow),
                    high_low(own_small),
                    pad,
                ],
                axis=0,
            ),
            step,
        ).astype(wide)
        up_bias_row = jnp.pad(bias_of(target), (0, channels - share))[None]
        up_got = across(
            jnp.concatenate(
                [
                    contract(grad_share, conv_rows, target).astype(narrow),
                    high_low(up_bias_row),
                    jnp.zeros((14, channels), narrow),
                ],
                axis=0,
            ),
            step,
        ).astype(wide)
        grad_down = grad_down + down_got[:share]
        small = small + down_got[share : share + 4] + down_got[share + 4 : share + 8]
        grad_up = grad_up + up_got[:share]
        grad_up_bias = grad_up_bias + (up_got[share] + up_got[share + 1])[:share]
    return (out_tokens, grad_down, grad_up, grad_up_bias, small[3], small[:3])


def solution(mesh):
    tokens = P(("groups", "tm", "tensor"), None)
    return jax.shard_map(
        local,
        mesh=mesh,
        in_specs=(tokens, tokens, P("tensor", None), P(), P(), P("tensor", None), P(), P()),
        out_specs=(
            tokens,
            tokens,
            tokens,
            P(("groups", "tm", "tensor")),
            P("groups"),
            P("groups", None),
        ),
        check_vma=False,
    )
```

```python
import functools

import jax
import jax.numpy as jnp
from jax import lax
from jax.experimental import pallas as pl
from jax.experimental.pallas import tpu as pltpu
from jax.sharding import PartitionSpec as P

epsilon = 1e-06
cores = 2
block_frames = 4
members = cores * block_frames
lanes = 128
chunk = 768
narrow, wide = jnp.bfloat16, jnp.float32


def inner_rows(left, right):
    return lax.dot_general(
        left, right, (((0,), (0,)), ((), ())), preferred_element_type=wide
    )


def outer_rows(left, right):
    return lax.dot_general(
        left, right, (((1,), (1,)), ((), ())), preferred_element_type=wide
    )


def folded(values):
    return sum(
        values[:, start : start + lanes] for start in range(0, values.shape[1], lanes)
    )


def lift_kernel(
    index_ref,
    frames_ref,
    cotangent_ref,
    conv_ref,
    own_ref,
    other_ref,
    bias_ref,
    gain_ref,
    out_ref,
    *other_refs,
):
    *sent_refs, grad_conv_ref, lifted_ref = other_refs
    tokens, features = frames_ref.shape
    half = features // cores
    share, half_blocks = sent_refs[0].shape[-1], sent_refs[0].shape[1] // cores
    core, place = index_ref[0], index_ref[1]
    conv = conv_ref[...]
    pieces = []
    for weight_ref, side in ((own_ref, core), (other_ref, 1 - core)):
        for start in range(0, half, chunk):
            pieces.append((weight_ref, start, side))

    def columns(start, side):
        return pl.ds(pl.multiple_of(side * half + start, lanes), chunk)

    total = jnp.zeros((tokens, lanes), wide)
    for weight_ref, start, side in pieces:
        where = columns(start, side)
        raised = outer_rows(conv, weight_ref[start : start + chunk, :])
        lifted = (frames_ref[:, where].astype(wide) + raised + bias_ref[:, where]).astype(narrow)
        lifted_ref[:, where] = lifted
        total = total + folded(lifted.astype(wide))
    center = jnp.sum(total, axis=1, keepdims=True) / features

    squares = jnp.zeros((tokens, lanes), wide)
    plain = jnp.zeros((tokens, lanes), wide)
    crossed = jnp.zeros((tokens, lanes), wide)
    for weight_ref, start, side in pieces:
        where = columns(start, side)
        shifted = lifted_ref[:, where].astype(wide) - center
        scaled = cotangent_ref[:, where].astype(wide) * gain_ref[:, where]
        squares = squares + folded(shifted * shifted)
        plain = plain + folded(scaled)
        crossed = crossed + folded(scaled * shifted)
    inverse = lax.rsqrt(jnp.sum(squares, axis=1, keepdims=True) / features + epsilon)
    mean_plain = jnp.sum(plain, axis=1, keepdims=True) / features
    mean_crossed = inverse * jnp.sum(crossed, axis=1, keepdims=True) / features

    grad_conv = jnp.zeros(grad_conv_ref.shape, wide)
    for weight_ref, start, side in pieces:
        where = columns(start, side)
        unit = (lifted_ref[:, where].astype(wide) - center) * inverse
        gain = gain_ref[:, where]
        out_ref[:, where] = (unit * gain).astype(narrow)
        scaled = cotangent_ref[:, where].astype(wide) * gain
        grad = (inverse * (scaled - mean_plain - unit * mean_crossed)).astype(narrow)
        for piece in range(chunk // share):
            slot = start // share + piece
            member, block = slot % members // cores, side * half_blocks + slot // members
            for step, sent_ref in enumerate(sent_refs):

                @pl.when((place ^ step) == member)
                def _():
                    sent_ref[core ^ (slot % cores), block] = grad[
                        :, piece * share : (piece + 1) * share
                    ]

        grad_conv = grad_conv + jnp.dot(
            grad, weight_ref[start : start + chunk, :], preferred_element_type=wide
        )
    grad_conv_ref[...] = grad_conv.astype(narrow)


def lift(index, frames_in, cotangent, conv, own, other, bias, gain, blocks, share):
    tokens, features = frames_in.shape
    channels = conv.shape[1]
    vmem = pl.BlockSpec(memory_space=pltpu.VMEM)
    return pl.pallas_call(
        lift_kernel,
        out_shape=(
            jax.ShapeDtypeStruct((tokens, features), narrow),
            *[jax.ShapeDtypeStruct((cores, blocks, tokens, share), narrow)] * block_frames,
            jax.ShapeDtypeStruct((tokens, channels), narrow),
        ),
        in_specs=[pl.BlockSpec(memory_space=pltpu.SMEM)] + [vmem] * 7,
        out_specs=(vmem,) * (2 + block_frames),
        scratch_shapes=[pltpu.VMEM((tokens, features), narrow)],
        compiler_params=pltpu.CompilerParams(vmem_limit_bytes=32 * 1024 * 1024),
        cost_estimate=pl.CostEstimate(
            flops=0,
            bytes_accessed=0,
            transcendentals=0,
        ),
        name="lift",
    )(index, frames_in, cotangent, conv, own, other, bias[None], gain[None])


def split_kernel(index_ref, value_ref, *out_refs):
    core, place = index_ref[0], index_ref[1]
    blocks, share = out_refs[0].shape[1], out_refs[0].shape[-1]
    for member in range(block_frames):
        for step in range(block_frames):

            @pl.when((place ^ step) == member)
            def _():
                for block in range(blocks):
                    for side in range(cores):
                        start = ((block * block_frames + member) * cores + side) * share
                        out_refs[step][core ^ side, block] = value_ref[:, start : start + share]


def split(index, value, blocks, share):
    vmem = pl.BlockSpec(memory_space=pltpu.VMEM)
    part = jax.ShapeDtypeStruct((cores, blocks, value.shape[0], share), value.dtype)
    return pl.pallas_call(
        split_kernel,
        out_shape=(part,) * block_frames,
        in_specs=[pl.BlockSpec(memory_space=pltpu.SMEM), vmem],
        out_specs=(vmem,) * block_frames,
        compiler_params=pltpu.CompilerParams(vmem_limit_bytes=16 * 1024 * 1024),
        name="split",
    )(index, value)


def squeeze_kernel(index_ref, frames_ref, weight_ref, start_ref, out_ref, *, side):
    half = weight_ref.shape[0]
    columns = pl.ds(pl.multiple_of((index_ref[0] ^ side) * half, lanes), half)
    total = start_ref[...] + jnp.dot(
        frames_ref[:, columns], weight_ref[...], preferred_element_type=wide
    )
    out_ref[...] = total.astype(out_ref.dtype)


def squeeze(index, frames_in, weight, start, side, dtype):
    vmem = pl.BlockSpec(memory_space=pltpu.VMEM)
    return pl.pallas_call(
        functools.partial(squeeze_kernel, side=side),
        out_shape=jax.ShapeDtypeStruct((frames_in.shape[0], weight.shape[1]), dtype),
        in_specs=[pl.BlockSpec(memory_space=pltpu.SMEM)] + [vmem] * 3,
        out_specs=vmem,
        compiler_params=pltpu.CompilerParams(vmem_limit_bytes=24 * 1024 * 1024),
        name="squeeze",
    )(index, frames_in, weight, start)


def block_frames_of(index_ref, refs):
    place, has_low, has_high = [index_ref[k] for k in range(3)]
    odd, upper = place % 2 == 1, place // 2 == 1
    parts = [ref[...].astype(wide) for ref in refs]
    low = [jnp.where(odd, parts[j ^ 1], parts[j]) for j in range(block_frames)]
    full = [jnp.where(upper, low[j ^ 2], low[j]) for j in range(block_frames)]
    before = jnp.where(has_low > 0, parts[block_frames], 0.0)
    behind = jnp.where(has_high > 0, parts[block_frames + 1], 0.0)
    return [before] + full + [behind]


def mix_grad_kernel(index_ref, taps_ref, *refs):
    earlier, same, later = [taps_ref[k : k + 1, :] for k in range(3)]
    per_core = block_frames + 2
    for side in range(cores):
        grads = block_frames_of(index_ref, refs[side * per_core : (side + 1) * per_core])
        for f in range(block_frames):
            mixed = earlier * grads[f + 2] + same * grads[f + 1] + later * grads[f]
            refs[-1][side, f ^ index_ref[0]] = mixed.astype(narrow)


def mix_conv_kernel(index_ref, taps_ref, grad_ref, *refs):
    earlier, same, later = [taps_ref[k : k + 1, :] for k in range(3)]
    per_core = block_frames + 2
    *inputs, conv_ref, small_ref = refs
    sums = [0.0] * 4
    for side in range(cores):
        bottles = block_frames_of(index_ref, inputs[side * per_core : (side + 1) * per_core])
        grads = inputs[cores * per_core + side * block_frames :][:block_frames]
        for f in range(block_frames):
            down, here, up = bottles[f : f + 3]
            conv_ref[side, f ^ index_ref[0]] = (
                earlier * down + same * here + later * up
            ).astype(narrow)
        for step in range(block_frames):
            grad = grads[step][...].astype(wide)
            f = index_ref[0] ^ step
            mixed = grad_ref[side, step].astype(wide)
            near = [
                sum(jnp.where(f == j, bottles[j + k], 0.0) for j in range(block_frames))
                for k in range(3)
            ]
            for k, value in enumerate([v * grad for v in near] + [mixed]):
                sums[k] = sums[k] + jnp.sum(value, axis=0, keepdims=True)
    small_ref[...] = jnp.zeros_like(small_ref)
    for k in range(4):
        small_ref[k : k + 1, :] = sums[k]


def mix(index, taps, parts, grad_rows=None):
    tokens, channels = parts[0].shape
    vmem = pl.BlockSpec(memory_space=pltpu.VMEM)
    rows = jax.ShapeDtypeStruct((cores, block_frames, tokens, channels), narrow)
    last = grad_rows is None
    operands = list(parts) if last else [grad_rows, *parts]
    return pl.pallas_call(
        mix_grad_kernel if last else mix_conv_kernel,
        out_shape=rows if last else (rows, jax.ShapeDtypeStruct((8, channels), wide)),
        in_specs=[pl.BlockSpec(memory_space=pltpu.SMEM)] + [vmem] * (1 + len(operands)),
        out_specs=vmem if last else (vmem, vmem),
        compiler_params=pltpu.CompilerParams(vmem_limit_bytes=24 * 1024 * 1024),
        name="mix_grad" if last else "mix_conv",
    )(index, taps, *operands)


def contract_kernel(targets_ref, rows_ref, small_ref, *refs):
    own, other = refs[:block_frames], refs[block_frames:members]
    total_ref, bias_ref, *sent_refs = refs[members:-1]
    extra_ref = refs[-1]
    share, channels = total_ref.shape

    def product(target):
        total = jnp.zeros((share, channels), wide)
        bias = jnp.zeros((1, share), wide)
        for step in range(block_frames):
            for side, value in ((0, own[step][0, target]), (1, other[step][target])):
                total = total + inner_rows(value, rows_ref[side, step])
                bias = bias + jnp.sum(value.astype(wide), axis=0, keepdims=True)
        return total, bias

    for index, sent_ref in enumerate(sent_refs):
        total, bias = product(targets_ref[index + 1])
        sent_ref[:share, :] = total.astype(narrow)
        if small_ref is not None:
            extra_ref[...] = jnp.zeros_like(extra_ref)
            extra_ref[0:4, :] = small_ref[0:4, :]
            extra_ref[4:5, :share] = bias
            high = extra_ref[0:8, :].astype(narrow).astype(wide)
            extra_ref[8:16, :] = extra_ref[0:8, :] - high
            sent_ref[share:, :] = extra_ref[...].astype(narrow)
    total_ref[...], bias_ref[...] = product(targets_ref[0])


def contract(targets, rows, small, parts):
    share, channels = parts[0].shape[-1], rows.shape[-1]
    blocks = parts[0].shape[1]
    vmem = pl.BlockSpec(memory_space=pltpu.VMEM)
    body = contract_kernel
    operands = [targets, rows] + ([] if small is None else [small]) + list(parts)
    if small is None:
        body = lambda targets_ref, rows_ref, *refs: contract_kernel(
            targets_ref, rows_ref, None, *refs
        )
    sent = jax.ShapeDtypeStruct((share + (0 if small is None else 16), channels), narrow)
    return pl.pallas_call(
        body,
        out_shape=(
            jax.ShapeDtypeStruct((share, channels), wide),
            jax.ShapeDtypeStruct((1, share), wide),
        )
        + (sent,) * (blocks - 1),
        in_specs=[pl.BlockSpec(memory_space=pltpu.SMEM)] + [vmem] * (len(operands) - 1),
        out_specs=(vmem,) * (blocks + 1),
        scratch_shapes=[pltpu.VMEM((16, channels), wide)],
        compiler_params=pltpu.CompilerParams(vmem_limit_bytes=24 * 1024 * 1024),
        name="contract_down" if small is None else "contract_up",
    )(*operands)


def after(values, other):
    return list(lax.optimization_barrier((tuple(values), other))[0])


def local(frames_in, cotangent, down_weight, down_bias, conv_kernel, up_weight, up_bias, ln_gain):
    tokens, features = frames_in.shape
    channels = down_weight.shape[1]
    count = lax.axis_size("tm")
    blocks = count // block_frames
    share = features // (count * cores)
    frame, core = lax.axis_index("tm"), lax.axis_index("tensor")
    block, place = frame // block_frames, frame % block_frames
    groups = [
        list(range(start, start + members)) for start in range(0, count * cores, members)
    ]

    def core_swap(value):
        return lax.ppermute(value, "tensor", [(0, 1), (1, 0)])

    def block_swap(value, step):
        return lax.ppermute(value, "tm", [(i, i ^ step) for i in range(count)])

    def to_members(value):
        return lax.all_to_all(
            value,
            ("tm", "tensor"),
            split_axis=0,
            concat_axis=0,
            tiled=True,
            axis_index_groups=groups,
        )

    def edge_swap(value):
        edges = range(block_frames - 1, count - 1, block_frames)
        return lax.ppermute(
            value, "tm", [p for i in edges for p in ((i, i + 1), (i + 1, i))]
        )

    def across(value, step):
        return lax.ppermute(
            value, "tm", [(i, (i + step * block_frames) % count) for i in range(count)]
        )

    def shifted(value, step):
        pairs = [(i, i + step * block_frames) for i in range(count)]
        return lax.ppermute(value, "tm", [p for p in pairs if 0 <= p[1] < count])

    def ordered(parts):
        low = [
            jnp.where(place % 2 == 1, parts[j ^ 1], parts[j]) for j in range(block_frames)
        ]
        return [jnp.where(place // 2 == 1, low[j ^ 2], low[j]) for j in range(block_frames)]

    index = jnp.stack([core, place]).astype(jnp.int32)
    down_other = core_swap(down_weight)
    frames_parts = list(
        split(index, frames_in, blocks, share)
    )
    index_after = after([index], frames_parts[3])[0]
    for step in (1, 2):
        frames_parts[step] = block_swap(frames_parts[step], step)
    bottle = squeeze(index_after, frames_in, down_weight, down_bias[None], 0, wide)
    bottle = squeeze(index, frames_in, down_other, bottle, 1, narrow)
    up_other = core_swap(up_weight)
    bottle_parts = [bottle] + [block_swap(bottle, step) for step in range(1, block_frames)]
    bottle_edge = edge_swap(bottle)
    frames_parts[3] = block_swap(
        after([frames_parts[3]], (bottle_parts[1:], bottle_edge))[0], 3
    )

    def pick(value, *places):
        chosen = sum([(place == p) for p in places[1:]], place == places[0])
        return jnp.where(chosen, value, 0.0)

    earlier, same, later = conv_kernel
    odd = place % 2 == 1
    conv = (
        jnp.where(odd, earlier, later) * bottle_parts[1].astype(wide)
        + same * bottle.astype(wide)
        + (pick(later, 1) + pick(earlier, 2)) * bottle_parts[3].astype(wide)
        + (pick(earlier, 0) + pick(later, 3)) * bottle_edge.astype(wide)
    ).astype(narrow)
    out_tokens, *grad_sent, grad_conv = lift(
        index,
        frames_in,
        cotangent,
        conv,
        up_weight,
        up_other,
        up_bias,
        ln_gain,
        blocks,
        share,
    )
    grad_conv, *grad_sent = after([grad_conv, *grad_sent], frames_parts[1:])
    grad_parts = [grad_conv] + [block_swap(grad_conv, step) for step in range(1, block_frames)]
    grad_sent = after(grad_sent, grad_parts[1])
    lifted_parts = [grad_sent[0]] + [
        block_swap(grad_sent[step], step) for step in range(1, block_frames)
    ]

    def by_core(parts):
        return list(parts) + [core_swap(v[1]) for v in parts]

    frames_got = by_core(after(frames_parts, grad_parts[1]))

    def whole_block(parts):
        if blocks == 2:
            beside = across(
                lax.select_n(jnp.where(block == 0, block_frames - 1, 0) ^ place, *parts), 1
            )
            sides = [beside, beside]
        else:
            frames = ordered(parts)
            sides = [shifted(frames[-1], 1), shifted(frames[0], -1)]
        own = list(parts) + sides[: 1 if blocks == 2 else 2]
        other = [core_swap(value) for value in own]
        return own[:block_frames] + sides, other[:block_frames] + [other[block_frames], other[-1]]

    grad_own, grad_other = whole_block(grad_parts)
    ends = jnp.stack([place, block, blocks - 1 - block]).astype(jnp.int32)
    grad_bottle = mix(ends, conv_kernel, after(grad_own + grad_other, lifted_parts[1:3]))
    targets = jnp.stack([(block + step) % blocks for step in range(blocks)]).astype(jnp.int32)
    grad_down, _, *down_sent = contract(targets, grad_bottle, None, frames_got)
    down_sent = after(down_sent, lifted_parts[3])
    down_got = [across(value, step + 1) for step, value in enumerate(down_sent)]
    bottle_own, bottle_other = whole_block(after(bottle_parts, lifted_parts[2]))
    conv_rows, small = mix(
        ends,
        conv_kernel,
        bottle_own + bottle_other + grad_own[:block_frames] + grad_other[:block_frames],
        grad_bottle,
    )
    grad_up, grad_up_bias, *up_sent = contract(targets, conv_rows, small, by_core(lifted_parts))
    up_got = [across(value, step + 1) for step, value in enumerate(up_sent)]
    down_got = after(down_got, up_sent[0])
    grad_up_bias, small = grad_up_bias[0], small[:5]
    small = small.at[4, :share].set(grad_up_bias)
    for down, up in zip(down_got, up_got):
        down, up = down.astype(wide), up.astype(wide)
        grad_down = grad_down + down[:share]
        grad_up = grad_up + up[:share]
        small = small + up[share : share + 5] + up[share + 8 : share + 13]
    grad_up_bias = small[4, :share]
    return (out_tokens, grad_down, grad_up, grad_up_bias, small[3], small[:3])


def solution(mesh):
    tokens = P(("groups", "tm", "tensor"), None)
    return jax.shard_map(
        local,
        mesh=mesh,
        in_specs=(tokens, tokens, P("tensor", None), P(), P(), P("tensor", None), P(), P()),
        out_specs=(
            tokens,
            tokens,
            tokens,
            P(("groups", "tm", "tensor")),
            P("groups"),
            P("groups", None),
        ),
        check_vma=False,
    )
```

```python
import functools

import jax
import jax.numpy as jnp
from jax import lax
from jax.experimental import pallas as pl
from jax.experimental.pallas import tpu as pltpu
from jax.sharding import PartitionSpec as P

epsilon = 1e-06
cores = 2
block_frames = 4
members = cores * block_frames
lanes = 128
chunk = 768
narrow, wide = jnp.bfloat16, jnp.float32


def inner_rows(left, right):
    return lax.dot_general(
        left, right, (((0,), (0,)), ((), ())), preferred_element_type=wide
    )


def outer_rows(left, right):
    return lax.dot_general(
        left, right, (((1,), (1,)), ((), ())), preferred_element_type=wide
    )


def folded(values):
    return sum(
        values[:, start : start + lanes] for start in range(0, values.shape[1], lanes)
    )


def lift_kernel(
    index_ref,
    frames_hbm,
    cotangent_hbm,
    conv_ref,
    own_hbm,
    other_hbm,
    vectors_ref,
    out_hbm,
    *refs,
):
    sent_hbm, grad_conv_ref = refs[:block_frames], refs[block_frames]
    (
        frames_ref,
        lifted_ref,
        cotangent_ref,
        own_ref,
        other_ref,
        out_ref,
        sent_ref,
        in_sems,
        out_sems,
    ) = refs[block_frames + 1 :]
    tokens, features = frames_ref.shape
    half = features // cores
    share, half_blocks = sent_ref.shape[-1], sent_ref.shape[2] // cores
    core, place = index_ref[0], index_ref[1]
    conv = conv_ref[...]
    def columns(start, side):
        return pl.ds(pl.multiple_of(side * half + start, lanes), chunk)

    pieces, loads = [], []
    for weight_hbm, weight_ref, side in (
        (other_hbm, other_ref, 1 - core),
        (own_hbm, own_ref, core),
    ):
        for start in range(0, half, chunk):
            where, rows, slot = columns(start, side), pl.ds(start, chunk), 2 * len(pieces)
            pieces.append((weight_ref, start, side))
            pair = (
                pltpu.make_async_copy(
                    weight_hbm.at[rows, :], weight_ref.at[rows, :], in_sems.at[slot]
                ),
                pltpu.make_async_copy(
                    frames_hbm.at[:, where], frames_ref.at[:, where], in_sems.at[slot + 1]
                ),
            )
            loads.append(pair)
            for copy in pair:
                copy.start()
    load = pltpu.make_async_copy(cotangent_hbm, cotangent_ref, in_sems.at[2 * len(pieces)])
    load.start()

    total = jnp.zeros((tokens, lanes), wide)
    for number, (weight_ref, start, side) in enumerate(pieces):
        for copy in loads[number]:
            copy.wait()
        where = columns(start, side)
        raised = outer_rows(conv, weight_ref[start : start + chunk, :])
        lifted = (frames_ref[:, where].astype(wide) + raised + vectors_ref[0:1, where]).astype(narrow)
        lifted_ref[:, where] = lifted
        total = total + folded(lifted.astype(wide))
    center = jnp.sum(total, axis=1, keepdims=True) / features

    load.wait()
    squares = jnp.zeros((tokens, lanes), wide)
    plain = jnp.zeros((tokens, lanes), wide)
    crossed = jnp.zeros((tokens, lanes), wide)
    for weight_ref, start, side in pieces:
        where = columns(start, side)
        shifted = lifted_ref[:, where].astype(wide) - center
        scaled = cotangent_ref[:, where].astype(wide) * vectors_ref[1:2, where]
        squares = squares + folded(shifted * shifted)
        plain = plain + folded(scaled)
        crossed = crossed + folded(scaled * shifted)
    inverse = lax.rsqrt(jnp.sum(squares, axis=1, keepdims=True) / features + epsilon)
    mean_plain = jnp.sum(plain, axis=1, keepdims=True) / features
    mean_crossed = inverse * jnp.sum(crossed, axis=1, keepdims=True) / features

    grad_conv = jnp.zeros(grad_conv_ref.shape, wide)
    stores = []
    for number, (weight_ref, start, side) in enumerate(pieces):
        where = columns(start, side)
        unit = (lifted_ref[:, where].astype(wide) - center) * inverse
        gain = vectors_ref[1:2, where]
        out_ref[:, where] = (unit * gain).astype(narrow)
        stores.append(
            pltpu.make_async_copy(
                out_ref.at[:, where], out_hbm.at[:, where], out_sems.at[block_frames + number]
            )
        )
        stores[-1].start()
        scaled = cotangent_ref[:, where].astype(wide) * gain
        grad = (inverse * (scaled - mean_plain - unit * mean_crossed)).astype(narrow)
        for piece in range(chunk // share):
            slot = start // share + piece
            member, block = slot % members // cores, side * half_blocks + slot // members
            sent_ref[place ^ member, core ^ (slot % cores), block] = grad[
                :, piece * share : (piece + 1) * share
            ]
        grad_conv = grad_conv + jnp.dot(
            grad, weight_ref[start : start + chunk, :], preferred_element_type=wide
        )
    for step in range(block_frames):
        stores.append(
            pltpu.make_async_copy(sent_ref.at[step], sent_hbm[step], out_sems.at[step])
        )
        stores[-1].start()
    grad_conv_ref[...] = grad_conv.astype(narrow)
    for copy in stores:
        copy.wait()


def lift(index, frames_in, cotangent, conv, own, other, bias, gain, blocks, share):
    tokens, features = frames_in.shape
    channels = conv.shape[1]
    vmem = pl.BlockSpec(memory_space=pltpu.VMEM)
    hbm = pl.BlockSpec(memory_space=pltpu.HBM)
    return pl.pallas_call(
        lift_kernel,
        out_shape=(
            jax.ShapeDtypeStruct((tokens, features), narrow),
            *[jax.ShapeDtypeStruct((cores, blocks, tokens, share), narrow)] * block_frames,
            jax.ShapeDtypeStruct((tokens, channels), narrow),
        ),
        in_specs=[pl.BlockSpec(memory_space=pltpu.SMEM), hbm, hbm, vmem, hbm, hbm, vmem],
        out_specs=(hbm,) * (1 + block_frames) + (vmem,),
        scratch_shapes=[
            pltpu.VMEM((tokens, features), narrow),
            pltpu.VMEM((tokens, features), narrow),
            pltpu.VMEM((tokens, features), narrow),
            pltpu.VMEM(own.shape, narrow),
            pltpu.VMEM(own.shape, narrow),
            pltpu.VMEM((tokens, features), narrow),
            pltpu.VMEM((block_frames, cores, blocks, tokens, share), narrow),
            pltpu.SemaphoreType.DMA((1 + 2 * (features // chunk),)),
            pltpu.SemaphoreType.DMA((block_frames + features // chunk,)),
        ],
        compiler_params=pltpu.CompilerParams(vmem_limit_bytes=60 * 1024 * 1024),
        cost_estimate=pl.CostEstimate(
            flops=0,
            bytes_accessed=0,
            transcendentals=0,
        ),
        name="lift",
    )(index, frames_in, cotangent, conv, own, other, jnp.stack([bias, gain]))


def split_kernel(index_ref, value_ref, *out_refs):
    core, place = index_ref[0], index_ref[1]
    blocks, share = out_refs[0].shape[1], out_refs[0].shape[-1]
    for member in range(block_frames):
        for step in range(block_frames):

            @pl.when((place ^ step) == member)
            def _():
                for block in range(blocks):
                    for side in range(cores):
                        start = ((block * block_frames + member) * cores + side) * share
                        out_refs[step][core ^ side, block] = value_ref[:, start : start + share]


def split(index, value, blocks, share):
    vmem = pl.BlockSpec(memory_space=pltpu.VMEM)
    part = jax.ShapeDtypeStruct((cores, blocks, value.shape[0], share), value.dtype)
    return pl.pallas_call(
        split_kernel,
        out_shape=(part,) * block_frames,
        in_specs=[pl.BlockSpec(memory_space=pltpu.SMEM), vmem],
        out_specs=(vmem,) * block_frames,
        compiler_params=pltpu.CompilerParams(vmem_limit_bytes=16 * 1024 * 1024),
        name="split",
    )(index, value)


def squeeze_kernel(index_ref, frames_ref, weight_ref, start_ref, out_ref, *, side):
    half = weight_ref.shape[0]
    columns = pl.ds(pl.multiple_of((index_ref[0] ^ side) * half, lanes), half)
    total = start_ref[...] + jnp.dot(
        frames_ref[:, columns], weight_ref[...], preferred_element_type=wide
    )
    out_ref[...] = total.astype(out_ref.dtype)


def squeeze(index, frames_in, weight, start, side, dtype):
    vmem = pl.BlockSpec(memory_space=pltpu.VMEM)
    return pl.pallas_call(
        functools.partial(squeeze_kernel, side=side),
        out_shape=jax.ShapeDtypeStruct((frames_in.shape[0], weight.shape[1]), dtype),
        in_specs=[pl.BlockSpec(memory_space=pltpu.SMEM)] + [vmem] * 3,
        out_specs=vmem,
        compiler_params=pltpu.CompilerParams(vmem_limit_bytes=24 * 1024 * 1024),
        name="squeeze",
    )(index, frames_in, weight, start)


def block_frames_of(index_ref, refs):
    place, has_low, has_high = [index_ref[k] for k in range(3)]
    odd, upper = place % 2 == 1, place // 2 == 1
    parts = [ref[...].astype(wide) for ref in refs]
    low = [jnp.where(odd, parts[j ^ 1], parts[j]) for j in range(block_frames)]
    full = [jnp.where(upper, low[j ^ 2], low[j]) for j in range(block_frames)]
    before = jnp.where(has_low > 0, parts[block_frames], 0.0)
    behind = jnp.where(has_high > 0, parts[block_frames + 1], 0.0)
    return [before] + full + [behind]


def mix_grad_kernel(index_ref, taps_ref, *refs):
    earlier, same, later = [taps_ref[k : k + 1, :] for k in range(3)]
    per_core = block_frames + 2
    for side in range(cores):
        grads = block_frames_of(index_ref, refs[side * per_core : (side + 1) * per_core])
        for f in range(block_frames):
            mixed = earlier * grads[f + 2] + same * grads[f + 1] + later * grads[f]
            refs[-1][side, f ^ index_ref[0]] = mixed.astype(narrow)


def mix_conv_kernel(index_ref, taps_ref, grad_ref, *refs):
    earlier, same, later = [taps_ref[k : k + 1, :] for k in range(3)]
    per_core = block_frames + 2
    *inputs, conv_ref, small_ref = refs
    sums = [0.0] * 4
    for side in range(cores):
        bottles = block_frames_of(index_ref, inputs[side * per_core : (side + 1) * per_core])
        grads = inputs[cores * per_core + side * block_frames :][:block_frames]
        for f in range(block_frames):
            down, here, up = bottles[f : f + 3]
            conv_ref[side, f ^ index_ref[0]] = (
                earlier * down + same * here + later * up
            ).astype(narrow)
        for step in range(block_frames):
            grad = grads[step][...].astype(wide)
            f = index_ref[0] ^ step
            mixed = grad_ref[side, step].astype(wide)
            near = [
                sum(jnp.where(f == j, bottles[j + k], 0.0) for j in range(block_frames))
                for k in range(3)
            ]
            for k, value in enumerate([v * grad for v in near] + [mixed]):
                sums[k] = sums[k] + jnp.sum(value, axis=0, keepdims=True)
    small_ref[...] = jnp.zeros_like(small_ref)
    for k in range(4):
        small_ref[k : k + 1, :] = sums[k]


def mix(index, taps, parts, grad_rows=None):
    tokens, channels = parts[0].shape
    vmem = pl.BlockSpec(memory_space=pltpu.VMEM)
    rows = jax.ShapeDtypeStruct((cores, block_frames, tokens, channels), narrow)
    last = grad_rows is None
    operands = list(parts) if last else [grad_rows, *parts]
    return pl.pallas_call(
        mix_grad_kernel if last else mix_conv_kernel,
        out_shape=rows if last else (rows, jax.ShapeDtypeStruct((8, channels), wide)),
        in_specs=[pl.BlockSpec(memory_space=pltpu.SMEM)] + [vmem] * (1 + len(operands)),
        out_specs=vmem if last else (vmem, vmem),
        compiler_params=pltpu.CompilerParams(vmem_limit_bytes=24 * 1024 * 1024),
        name="mix_grad" if last else "mix_conv",
    )(index, taps, *operands)


def contract_kernel(targets_ref, rows_ref, small_ref, *refs):
    own, other = refs[:block_frames], refs[block_frames:members]
    total_ref, bias_ref, *sent_refs = refs[members:-1]
    extra_ref = refs[-1]
    share, channels = total_ref.shape

    def product(target):
        total = jnp.zeros((share, channels), wide)
        bias = jnp.zeros((1, share), wide)
        for step in range(block_frames):
            for side, value in ((0, own[step][0, target]), (1, other[step][target])):
                total = total + inner_rows(value, rows_ref[side, step])
                bias = bias + jnp.sum(value.astype(wide), axis=0, keepdims=True)
        return total, bias

    for index, sent_ref in enumerate(sent_refs):
        total, bias = product(targets_ref[index + 1])
        sent_ref[:share, :] = total.astype(narrow)
        if small_ref is not None:
            extra_ref[...] = jnp.zeros_like(extra_ref)
            extra_ref[0:4, :] = small_ref[0:4, :]
            extra_ref[4:5, :share] = bias
            high = extra_ref[0:8, :].astype(narrow).astype(wide)
            extra_ref[8:16, :] = extra_ref[0:8, :] - high
            sent_ref[share:, :] = extra_ref[...].astype(narrow)
    total_ref[...], bias_ref[...] = product(targets_ref[0])


def contract(targets, rows, small, parts):
    share, channels = parts[0].shape[-1], rows.shape[-1]
    blocks = parts[0].shape[1]
    vmem = pl.BlockSpec(memory_space=pltpu.VMEM)
    body = contract_kernel
    operands = [targets, rows] + ([] if small is None else [small]) + list(parts)
    if small is None:
        body = lambda targets_ref, rows_ref, *refs: contract_kernel(
            targets_ref, rows_ref, None, *refs
        )
    sent = jax.ShapeDtypeStruct((share + (0 if small is None else 16), channels), narrow)
    return pl.pallas_call(
        body,
        out_shape=(
            jax.ShapeDtypeStruct((share, channels), wide),
            jax.ShapeDtypeStruct((1, share), wide),
        )
        + (sent,) * (blocks - 1),
        in_specs=[pl.BlockSpec(memory_space=pltpu.SMEM)] + [vmem] * (len(operands) - 1),
        out_specs=(vmem,) * (blocks + 1),
        scratch_shapes=[pltpu.VMEM((16, channels), wide)],
        compiler_params=pltpu.CompilerParams(vmem_limit_bytes=24 * 1024 * 1024),
        name="contract_down" if small is None else "contract_up",
    )(*operands)


def after(values, other):
    return list(lax.optimization_barrier((tuple(values), other))[0])


def local(frames_in, cotangent, down_weight, down_bias, conv_kernel, up_weight, up_bias, ln_gain):
    tokens, features = frames_in.shape
    channels = down_weight.shape[1]
    count = lax.axis_size("tm")
    blocks = count // block_frames
    share = features // (count * cores)
    frame, core = lax.axis_index("tm"), lax.axis_index("tensor")
    block, place = frame // block_frames, frame % block_frames
    groups = [
        list(range(start, start + members)) for start in range(0, count * cores, members)
    ]

    def core_swap(value):
        return lax.ppermute(value, "tensor", [(0, 1), (1, 0)])

    def block_swap(value, step):
        return lax.ppermute(value, "tm", [(i, i ^ step) for i in range(count)])

    def to_members(value):
        return lax.all_to_all(
            value,
            ("tm", "tensor"),
            split_axis=0,
            concat_axis=0,
            tiled=True,
            axis_index_groups=groups,
        )

    def edge_swap(value):
        edges = range(block_frames - 1, count - 1, block_frames)
        return lax.ppermute(
            value, "tm", [p for i in edges for p in ((i, i + 1), (i + 1, i))]
        )

    def across(value, step):
        return lax.ppermute(
            value, "tm", [(i, (i + step * block_frames) % count) for i in range(count)]
        )

    def shifted(value, step):
        pairs = [(i, i + step * block_frames) for i in range(count)]
        return lax.ppermute(value, "tm", [p for p in pairs if 0 <= p[1] < count])

    def ordered(parts):
        low = [
            jnp.where(place % 2 == 1, parts[j ^ 1], parts[j]) for j in range(block_frames)
        ]
        return [jnp.where(place // 2 == 1, low[j ^ 2], low[j]) for j in range(block_frames)]

    index = jnp.stack([core, place]).astype(jnp.int32)
    down_other = core_swap(down_weight)
    frames_parts = list(
        split(index, frames_in, blocks, share)
    )
    index_after = after([index], frames_parts[3])[0]
    for step in (1, 2):
        frames_parts[step] = block_swap(frames_parts[step], step)
    bottle = squeeze(index_after, frames_in, down_weight, down_bias[None], 0, wide)
    bottle = squeeze(index, frames_in, down_other, bottle, 1, narrow)
    bottle = after([bottle], frames_parts[1:3])[0]
    up_other = core_swap(up_weight)
    bottle_edge = edge_swap(bottle)
    bottle_parts = [
        bottle,
        block_swap(bottle, 1),
        block_swap(after([bottle], bottle_edge)[0], 2),
        block_swap(bottle, 3),
    ]
    frames_parts[3] = block_swap(
        after([frames_parts[3]], (bottle_parts[1], bottle_parts[3], bottle_edge))[0], 3
    )

    def pick(value, *places):
        chosen = sum([(place == p) for p in places[1:]], place == places[0])
        return jnp.where(chosen, value, 0.0)

    earlier, same, later = conv_kernel
    odd = place % 2 == 1
    conv = (
        jnp.where(odd, earlier, later) * bottle_parts[1].astype(wide)
        + same * bottle.astype(wide)
        + (pick(later, 1) + pick(earlier, 2)) * bottle_parts[3].astype(wide)
        + (pick(earlier, 0) + pick(later, 3)) * bottle_edge.astype(wide)
    ).astype(narrow)
    out_tokens, *grad_sent, grad_conv = lift(
        index,
        frames_in,
        cotangent,
        conv,
        up_weight,
        up_other,
        up_bias,
        ln_gain,
        blocks,
        share,
    )
    grad_conv, *grad_sent = after([grad_conv, *grad_sent], frames_parts[1:])
    grad_parts = [grad_conv] + [block_swap(grad_conv, step) for step in range(1, block_frames)]
    grad_sent = after(grad_sent, grad_parts[1])
    lifted_parts = [grad_sent[0]] + [
        block_swap(grad_sent[step], step) for step in range(1, block_frames)
    ]

    def by_core(parts):
        return list(parts) + [core_swap(v[1]) for v in parts]

    frames_got = by_core(after(frames_parts, grad_parts[1]))

    def whole_block(parts, late):
        if blocks == 2:
            beside = across(
                lax.select_n(jnp.where(block == 0, block_frames - 1, 0) ^ place, *parts), 1
            )
            sides = [beside, beside]
        else:
            frames = ordered(parts)
            sides = [shifted(frames[-1], 1), shifted(frames[0], -1)]
        if late is not None:
            sides = after(sides, late)
        own = list(parts) + sides[: 1 if blocks == 2 else 2]
        other = [core_swap(value) for value in own]
        return own[:block_frames] + sides, other[:block_frames] + [other[block_frames], other[-1]]

    grad_own, grad_other = whole_block(grad_parts, None)
    ends = jnp.stack([place, block, blocks - 1 - block]).astype(jnp.int32)
    grad_bottle = mix(ends, conv_kernel, after(grad_own + grad_other, lifted_parts[1:3]))
    targets = jnp.stack([(block + step) % blocks for step in range(blocks)]).astype(jnp.int32)
    grad_down, _, *down_sent = contract(targets, grad_bottle, None, frames_got)
    bottle_own, bottle_other = whole_block(
        after(bottle_parts, grad_parts[3]), lifted_parts[2]
    )
    conv_rows, small = mix(
        ends,
        conv_kernel,
        bottle_own + bottle_other + grad_own[:block_frames] + grad_other[:block_frames],
        grad_bottle,
    )
    down_got = [across(value, step + 1) for step, value in enumerate(down_sent)]
    grad_up, grad_up_bias, *up_sent = contract(targets, conv_rows, small, by_core(lifted_parts))
    up_got = [across(value, step + 1) for step, value in enumerate(up_sent)]
    down_got = after(down_got, up_sent[0])
    grad_up_bias, small = grad_up_bias[0], small[:5]
    small = small.at[4, :share].set(grad_up_bias)
    for down, up in zip(down_got, up_got):
        down, up = down.astype(wide), up.astype(wide)
        grad_down = grad_down + down[:share]
        grad_up = grad_up + up[:share]
        small = small + up[share : share + 5] + up[share + 8 : share + 13]
    grad_up_bias = small[4, :share]
    return (out_tokens, grad_down, grad_up, grad_up_bias, small[3], small[:3])


def solution(mesh):
    tokens = P(("groups", "tm", "tensor"), None)
    return jax.shard_map(
        local,
        mesh=mesh,
        in_specs=(tokens, tokens, P("tensor", None), P(), P(), P("tensor", None), P(), P()),
        out_specs=(
            tokens,
            tokens,
            tokens,
            P(("groups", "tm", "tensor")),
            P("groups"),
            P("groups", None),
        ),
        check_vma=False,
    )
```

```python
import functools

import jax
import jax.numpy as jnp
from jax import lax
from jax.experimental import pallas as pl
from jax.experimental.pallas import tpu as pltpu
from jax.sharding import PartitionSpec as P

epsilon = 1e-06
cores = 2
block_frames = 4
members = cores * block_frames
lanes = 128
chunk = 1536
narrow, wide = jnp.bfloat16, jnp.float32


def inner_rows(left, right):
    return lax.dot_general(
        left, right, (((0,), (0,)), ((), ())), preferred_element_type=wide
    )


def outer_rows(left, right):
    return lax.dot_general(
        left, right, (((1,), (1,)), ((), ())), preferred_element_type=wide
    )


def folded(values):
    return sum(
        values[:, start : start + lanes] for start in range(0, values.shape[1], lanes)
    )


def lift_kernel(
    index_ref,
    frames_hbm,
    cotangent_hbm,
    conv_ref,
    own_hbm,
    other_hbm,
    vectors_ref,
    out_hbm,
    *refs,
):
    sent_hbm, grad_conv_ref = refs[:block_frames], refs[block_frames]
    (
        frames_ref,
        lifted_ref,
        cotangent_ref,
        own_ref,
        other_ref,
        out_ref,
        sent_ref,
        in_sems,
        out_sems,
    ) = refs[block_frames + 1 :]
    tokens, features = frames_ref.shape
    half = features // cores
    share, half_blocks = sent_ref.shape[-1], sent_ref.shape[2] // cores
    core, place = index_ref[0], index_ref[1]
    conv = conv_ref[...]
    def columns(start, side):
        return pl.ds(pl.multiple_of(side * half + start, lanes), chunk)

    pieces, loads = [], []
    for weight_hbm, weight_ref, side in (
        (other_hbm, other_ref, 1 - core),
        (own_hbm, own_ref, core),
    ):
        for start in range(0, half, chunk):
            where, rows, slot = columns(start, side), pl.ds(start, chunk), 2 * len(pieces)
            pieces.append((weight_ref, start, side))
            pair = (
                pltpu.make_async_copy(
                    weight_hbm.at[rows, :], weight_ref.at[rows, :], in_sems.at[slot]
                ),
                pltpu.make_async_copy(
                    frames_hbm.at[:, where], frames_ref.at[:, where], in_sems.at[slot + 1]
                ),
            )
            loads.append(pair)
            for copy in pair:
                copy.start()
    load = pltpu.make_async_copy(cotangent_hbm, cotangent_ref, in_sems.at[2 * len(pieces)])
    load.start()

    total = jnp.zeros((tokens, lanes), wide)
    for number, (weight_ref, start, side) in enumerate(pieces):
        for copy in loads[number]:
            copy.wait()
        where = columns(start, side)
        raised = outer_rows(conv, weight_ref[start : start + chunk, :])
        lifted = (frames_ref[:, where].astype(wide) + raised + vectors_ref[0:1, where]).astype(narrow)
        lifted_ref[:, where] = lifted
        total = total + folded(lifted.astype(wide))
    center = jnp.sum(total, axis=1, keepdims=True) / features

    load.wait()
    squares = jnp.zeros((tokens, lanes), wide)
    plain = jnp.zeros((tokens, lanes), wide)
    crossed = jnp.zeros((tokens, lanes), wide)
    for weight_ref, start, side in pieces:
        where = columns(start, side)
        shifted = lifted_ref[:, where].astype(wide) - center
        scaled = cotangent_ref[:, where].astype(wide) * vectors_ref[1:2, where]
        squares = squares + folded(shifted * shifted)
        plain = plain + folded(scaled)
        crossed = crossed + folded(scaled * shifted)
    inverse = lax.rsqrt(jnp.sum(squares, axis=1, keepdims=True) / features + epsilon)
    mean_plain = jnp.sum(plain, axis=1, keepdims=True) / features
    mean_crossed = inverse * jnp.sum(crossed, axis=1, keepdims=True) / features

    grad_conv = jnp.zeros(grad_conv_ref.shape, wide)
    stores = []
    for number, (weight_ref, start, side) in enumerate(pieces):
        where = columns(start, side)
        unit = (lifted_ref[:, where].astype(wide) - center) * inverse
        gain = vectors_ref[1:2, where]
        out_ref[:, where] = (unit * gain).astype(narrow)
        stores.append(
            pltpu.make_async_copy(
                out_ref.at[:, where], out_hbm.at[:, where], out_sems.at[block_frames + number]
            )
        )
        stores[-1].start()
        scaled = cotangent_ref[:, where].astype(wide) * gain
        grad = (inverse * (scaled - mean_plain - unit * mean_crossed)).astype(narrow)
        for piece in range(chunk // share):
            slot = start // share + piece
            member, block = slot % members // cores, side * half_blocks + slot // members
            sent_ref[place ^ member, core ^ (slot % cores), block] = grad[
                :, piece * share : (piece + 1) * share
            ]
        grad_conv = grad_conv + jnp.dot(
            grad, weight_ref[start : start + chunk, :], preferred_element_type=wide
        )
    for step in range(block_frames):
        stores.append(
            pltpu.make_async_copy(sent_ref.at[step], sent_hbm[step], out_sems.at[step])
        )
        stores[-1].start()
    grad_conv_ref[...] = grad_conv.astype(narrow)
    for copy in stores:
        copy.wait()


def lift(index, frames_in, cotangent, conv, own, other, bias, gain, blocks, share):
    tokens, features = frames_in.shape
    channels = conv.shape[1]
    vmem = pl.BlockSpec(memory_space=pltpu.VMEM)
    hbm = pl.BlockSpec(memory_space=pltpu.HBM)
    return pl.pallas_call(
        lift_kernel,
        out_shape=(
            jax.ShapeDtypeStruct((tokens, features), narrow),
            *[jax.ShapeDtypeStruct((cores, blocks, tokens, share), narrow)] * block_frames,
            jax.ShapeDtypeStruct((tokens, channels), narrow),
        ),
        in_specs=[pl.BlockSpec(memory_space=pltpu.SMEM), hbm, hbm, vmem, hbm, hbm, vmem],
        out_specs=(hbm,) * (1 + block_frames) + (vmem,),
        scratch_shapes=[
            pltpu.VMEM((tokens, features), narrow),
            pltpu.VMEM((tokens, features), narrow),
            pltpu.VMEM((tokens, features), narrow),
            pltpu.VMEM(own.shape, narrow),
            pltpu.VMEM(own.shape, narrow),
            pltpu.VMEM((tokens, features), narrow),
            pltpu.VMEM((block_frames, cores, blocks, tokens, share), narrow),
            pltpu.SemaphoreType.DMA((1 + 2 * (features // chunk),)),
            pltpu.SemaphoreType.DMA((block_frames + features // chunk,)),
        ],
        compiler_params=pltpu.CompilerParams(vmem_limit_bytes=60 * 1024 * 1024),
        cost_estimate=pl.CostEstimate(
            flops=0,
            bytes_accessed=0,
            transcendentals=0,
        ),
        name="lift",
    )(index, frames_in, cotangent, conv, own, other, jnp.stack([bias, gain]))


def split_kernel(index_ref, value_ref, *out_refs):
    core, place = index_ref[0], index_ref[1]
    blocks, share = out_refs[0].shape[1], out_refs[0].shape[-1]
    for member in range(block_frames):
        for step in range(block_frames):

            @pl.when((place ^ step) == member)
            def _():
                for block in range(blocks):
                    for side in range(cores):
                        start = ((block * block_frames + member) * cores + side) * share
                        out_refs[step][core ^ side, block] = value_ref[:, start : start + share]


def split(index, value, blocks, share):
    vmem = pl.BlockSpec(memory_space=pltpu.VMEM)
    part = jax.ShapeDtypeStruct((cores, blocks, value.shape[0], share), value.dtype)
    return pl.pallas_call(
        split_kernel,
        out_shape=(part,) * block_frames,
        in_specs=[pl.BlockSpec(memory_space=pltpu.SMEM), vmem],
        out_specs=(vmem,) * block_frames,
        compiler_params=pltpu.CompilerParams(vmem_limit_bytes=16 * 1024 * 1024),
        name="split",
    )(index, value)


def squeeze_kernel(index_ref, frames_ref, weight_ref, start_ref, out_ref, *, side):
    half = weight_ref.shape[0]
    columns = pl.ds(pl.multiple_of((index_ref[0] ^ side) * half, lanes), half)
    total = start_ref[...] + jnp.dot(
        frames_ref[:, columns], weight_ref[...], preferred_element_type=wide
    )
    out_ref[...] = total.astype(out_ref.dtype)


def squeeze(index, frames_in, weight, start, side, dtype):
    vmem = pl.BlockSpec(memory_space=pltpu.VMEM)
    return pl.pallas_call(
        functools.partial(squeeze_kernel, side=side),
        out_shape=jax.ShapeDtypeStruct((frames_in.shape[0], weight.shape[1]), dtype),
        in_specs=[pl.BlockSpec(memory_space=pltpu.SMEM)] + [vmem] * 3,
        out_specs=vmem,
        compiler_params=pltpu.CompilerParams(vmem_limit_bytes=24 * 1024 * 1024),
        name="squeeze",
    )(index, frames_in, weight, start)


def block_frames_of(index_ref, refs):
    place, has_low, has_high = [index_ref[k] for k in range(3)]
    odd, upper = place % 2 == 1, place // 2 == 1
    parts = [ref[...].astype(wide) for ref in refs]
    low = [jnp.where(odd, parts[j ^ 1], parts[j]) for j in range(block_frames)]
    full = [jnp.where(upper, low[j ^ 2], low[j]) for j in range(block_frames)]
    before = jnp.where(has_low > 0, parts[block_frames], 0.0)
    behind = jnp.where(has_high > 0, parts[block_frames + 1], 0.0)
    return [before] + full + [behind]


def mix_grad_kernel(index_ref, taps_ref, *refs):
    earlier, same, later = [taps_ref[k : k + 1, :] for k in range(3)]
    per_core = block_frames + 2
    for side in range(cores):
        grads = block_frames_of(index_ref, refs[side * per_core : (side + 1) * per_core])
        for f in range(block_frames):
            mixed = earlier * grads[f + 2] + same * grads[f + 1] + later * grads[f]
            refs[-1][side, f ^ index_ref[0]] = mixed.astype(narrow)


def mix_conv_kernel(index_ref, taps_ref, grad_ref, *refs):
    earlier, same, later = [taps_ref[k : k + 1, :] for k in range(3)]
    per_core = block_frames + 2
    *inputs, conv_ref, small_ref = refs
    sums = [0.0] * 4
    for side in range(cores):
        bottles = block_frames_of(index_ref, inputs[side * per_core : (side + 1) * per_core])
        grads = inputs[cores * per_core + side * block_frames :][:block_frames]
        for f in range(block_frames):
            down, here, up = bottles[f : f + 3]
            conv_ref[side, f ^ index_ref[0]] = (
                earlier * down + same * here + later * up
            ).astype(narrow)
        for step in range(block_frames):
            grad = grads[step][...].astype(wide)
            f = index_ref[0] ^ step
            mixed = grad_ref[side, step].astype(wide)
            near = [
                sum(jnp.where(f == j, bottles[j + k], 0.0) for j in range(block_frames))
                for k in range(3)
            ]
            for k, value in enumerate([v * grad for v in near] + [mixed]):
                sums[k] = sums[k] + jnp.sum(value, axis=0, keepdims=True)
    small_ref[...] = jnp.zeros_like(small_ref)
    for k in range(4):
        small_ref[k : k + 1, :] = sums[k]


def mix(index, taps, parts, grad_rows=None):
    tokens, channels = parts[0].shape
    vmem = pl.BlockSpec(memory_space=pltpu.VMEM)
    rows = jax.ShapeDtypeStruct((cores, block_frames, tokens, channels), narrow)
    last = grad_rows is None
    operands = list(parts) if last else [grad_rows, *parts]
    return pl.pallas_call(
        mix_grad_kernel if last else mix_conv_kernel,
        out_shape=rows if last else (rows, jax.ShapeDtypeStruct((8, channels), wide)),
        in_specs=[pl.BlockSpec(memory_space=pltpu.SMEM)] + [vmem] * (1 + len(operands)),
        out_specs=vmem if last else (vmem, vmem),
        compiler_params=pltpu.CompilerParams(vmem_limit_bytes=24 * 1024 * 1024),
        name="mix_grad" if last else "mix_conv",
    )(index, taps, *operands)


def contract_kernel(targets_ref, rows_ref, small_ref, *refs):
    own, other = refs[:block_frames], refs[block_frames:members]
    total_ref, bias_ref, *sent_refs = refs[members:-1]
    extra_ref = refs[-1]
    share, channels = total_ref.shape

    def product(target):
        total = jnp.zeros((share, channels), wide)
        bias = jnp.zeros((1, share), wide)
        for step in range(block_frames):
            for side, value in ((0, own[step][0, target]), (1, other[step][target])):
                total = total + inner_rows(value, rows_ref[side, step])
                bias = bias + jnp.sum(value.astype(wide), axis=0, keepdims=True)
        return total, bias

    for index, sent_ref in enumerate(sent_refs):
        total, bias = product(targets_ref[index + 1])
        sent_ref[:share, :] = total.astype(narrow)
        if small_ref is not None:
            extra_ref[...] = jnp.zeros_like(extra_ref)
            extra_ref[0:4, :] = small_ref[0:4, :]
            extra_ref[4:5, :share] = bias
            high = extra_ref[0:8, :].astype(narrow).astype(wide)
            extra_ref[8:16, :] = extra_ref[0:8, :] - high
            sent_ref[share:, :] = extra_ref[...].astype(narrow)
    total_ref[...], bias_ref[...] = product(targets_ref[0])


def contract(targets, rows, small, parts):
    share, channels = parts[0].shape[-1], rows.shape[-1]
    blocks = parts[0].shape[1]
    vmem = pl.BlockSpec(memory_space=pltpu.VMEM)
    body = contract_kernel
    operands = [targets, rows] + ([] if small is None else [small]) + list(parts)
    if small is None:
        body = lambda targets_ref, rows_ref, *refs: contract_kernel(
            targets_ref, rows_ref, None, *refs
        )
    sent = jax.ShapeDtypeStruct((share + (0 if small is None else 16), channels), narrow)
    return pl.pallas_call(
        body,
        out_shape=(
            jax.ShapeDtypeStruct((share, channels), wide),
            jax.ShapeDtypeStruct((1, share), wide),
        )
        + (sent,) * (blocks - 1),
        in_specs=[pl.BlockSpec(memory_space=pltpu.SMEM)] + [vmem] * (len(operands) - 1),
        out_specs=(vmem,) * (blocks + 1),
        scratch_shapes=[pltpu.VMEM((16, channels), wide)],
        compiler_params=pltpu.CompilerParams(vmem_limit_bytes=24 * 1024 * 1024),
        name="contract_down" if small is None else "contract_up",
    )(*operands)


def after(values, other):
    return list(lax.optimization_barrier((tuple(values), other))[0])


def local(frames_in, cotangent, down_weight, down_bias, conv_kernel, up_weight, up_bias, ln_gain):
    tokens, features = frames_in.shape
    channels = down_weight.shape[1]
    count = lax.axis_size("tm")
    blocks = count // block_frames
    share = features // (count * cores)
    frame, core = lax.axis_index("tm"), lax.axis_index("tensor")
    block, place = frame // block_frames, frame % block_frames
    groups = [
        list(range(start, start + members)) for start in range(0, count * cores, members)
    ]

    def core_swap(value):
        return lax.ppermute(value, "tensor", [(0, 1), (1, 0)])

    def block_swap(value, step):
        return lax.ppermute(value, "tm", [(i, i ^ step) for i in range(count)])

    def to_members(value):
        return lax.all_to_all(
            value,
            ("tm", "tensor"),
            split_axis=0,
            concat_axis=0,
            tiled=True,
            axis_index_groups=groups,
        )

    def edge_swap(value):
        edges = range(block_frames - 1, count - 1, block_frames)
        return lax.ppermute(
            value, "tm", [p for i in edges for p in ((i, i + 1), (i + 1, i))]
        )

    def across(value, step):
        return lax.ppermute(
            value, "tm", [(i, (i + step * block_frames) % count) for i in range(count)]
        )

    def shifted(value, step):
        pairs = [(i, i + step * block_frames) for i in range(count)]
        return lax.ppermute(value, "tm", [p for p in pairs if 0 <= p[1] < count])

    def ordered(parts):
        low = [
            jnp.where(place % 2 == 1, parts[j ^ 1], parts[j]) for j in range(block_frames)
        ]
        return [jnp.where(place // 2 == 1, low[j ^ 2], low[j]) for j in range(block_frames)]

    index = jnp.stack([core, place]).astype(jnp.int32)
    down_other = core_swap(down_weight)
    frames_parts = list(
        split(index, frames_in, blocks, share)
    )
    index_after = after([index], frames_parts[3])[0]
    for step in (1, 2):
        frames_parts[step] = block_swap(frames_parts[step], step)
    bottle = squeeze(index_after, frames_in, down_weight, down_bias[None], 0, wide)
    bottle = squeeze(index, frames_in, down_other, bottle, 1, narrow)
    bottle = after([bottle], frames_parts[1:3])[0]
    up_other = core_swap(up_weight)
    bottle_edge = edge_swap(bottle)
    bottle_parts = [
        bottle,
        block_swap(bottle, 1),
        block_swap(after([bottle], bottle_edge)[0], 2),
        block_swap(bottle, 3),
    ]
    frames_parts[3] = block_swap(
        after([frames_parts[3]], (bottle_parts[1], bottle_parts[3], bottle_edge))[0], 3
    )

    def pick(value, *places):
        chosen = sum([(place == p) for p in places[1:]], place == places[0])
        return jnp.where(chosen, value, 0.0)

    earlier, same, later = conv_kernel
    odd = place % 2 == 1
    conv = (
        jnp.where(odd, earlier, later) * bottle_parts[1].astype(wide)
        + same * bottle.astype(wide)
        + (pick(later, 1) + pick(earlier, 2)) * bottle_parts[3].astype(wide)
        + (pick(earlier, 0) + pick(later, 3)) * bottle_edge.astype(wide)
    ).astype(narrow)
    out_tokens, *grad_sent, grad_conv = lift(
        index,
        frames_in,
        cotangent,
        conv,
        up_weight,
        up_other,
        up_bias,
        ln_gain,
        blocks,
        share,
    )
    grad_conv, *grad_sent = after([grad_conv, *grad_sent], frames_parts[1:])
    grad_parts = [grad_conv] + [block_swap(grad_conv, step) for step in range(1, block_frames)]
    grad_sent = after(grad_sent, grad_parts[1])
    lifted_parts = [grad_sent[0]] + [
        block_swap(grad_sent[step], step) for step in range(1, block_frames)
    ]

    def by_core(parts):
        return list(parts) + [core_swap(v[1]) for v in parts]

    frames_got = by_core(after(frames_parts, grad_parts[1]))

    def whole_block(parts, late):
        if blocks == 2:
            beside = across(
                lax.select_n(jnp.where(block == 0, block_frames - 1, 0) ^ place, *parts), 1
            )
            sides = [beside, beside]
        else:
            frames = ordered(parts)
            sides = [shifted(frames[-1], 1), shifted(frames[0], -1)]
        if late is not None:
            sides = after(sides, late)
        own = list(parts) + sides[: 1 if blocks == 2 else 2]
        other = [core_swap(value) for value in own]
        return own[:block_frames] + sides, other[:block_frames] + [other[block_frames], other[-1]]

    grad_own, grad_other = whole_block(grad_parts, None)
    ends = jnp.stack([place, block, blocks - 1 - block]).astype(jnp.int32)
    grad_bottle = mix(ends, conv_kernel, after(grad_own + grad_other, lifted_parts[1:3]))
    targets = jnp.stack([(block + step) % blocks for step in range(blocks)]).astype(jnp.int32)
    grad_down, _, *down_sent = contract(targets, grad_bottle, None, frames_got)
    bottle_own, bottle_other = whole_block(
        after(bottle_parts, grad_parts[3]), lifted_parts[2]
    )
    conv_rows, small = mix(
        ends,
        conv_kernel,
        bottle_own + bottle_other + grad_own[:block_frames] + grad_other[:block_frames],
        grad_bottle,
    )
    down_got = [across(value, step + 1) for step, value in enumerate(down_sent)]
    grad_up, grad_up_bias, *up_sent = contract(targets, conv_rows, small, by_core(lifted_parts))
    up_got = [across(value, step + 1) for step, value in enumerate(up_sent)]
    down_got = after(down_got, up_sent[0])
    grad_up_bias, small = grad_up_bias[0], small[:5]
    small = small.at[4, :share].set(grad_up_bias)
    for down, up in zip(down_got, up_got):
        down, up = down.astype(wide), up.astype(wide)
        grad_down = grad_down + down[:share]
        grad_up = grad_up + up[:share]
        small = small + up[share : share + 5] + up[share + 8 : share + 13]
    grad_up_bias = small[4, :share]
    return (out_tokens, grad_down, grad_up, grad_up_bias, small[3], small[:3])


def solution(mesh):
    tokens = P(("groups", "tm", "tensor"), None)
    return jax.shard_map(
        local,
        mesh=mesh,
        in_specs=(tokens, tokens, P("tensor", None), P(), P(), P("tensor", None), P(), P()),
        out_specs=(
            tokens,
            tokens,
            tokens,
            P(("groups", "tm", "tensor")),
            P("groups"),
            P("groups", None),
        ),
        check_vma=False,
    )
```

```python
import functools

import jax
import jax.numpy as jnp
from jax import lax
from jax.experimental import pallas as pl
from jax.experimental.pallas import tpu as pltpu
from jax.sharding import PartitionSpec as P

epsilon = 1e-06
cores = 2
block_frames = 4
members = cores * block_frames
lanes = 128
chunk = 3072
narrow, wide = jnp.bfloat16, jnp.float32


def inner_rows(left, right):
    return lax.dot_general(
        left, right, (((0,), (0,)), ((), ())), preferred_element_type=wide
    )


def outer_rows(left, right):
    return lax.dot_general(
        left, right, (((1,), (1,)), ((), ())), preferred_element_type=wide
    )


def folded(values):
    return sum(
        values[:, start : start + lanes] for start in range(0, values.shape[1], lanes)
    )


def lift_kernel(
    index_ref,
    frames_hbm,
    cotangent_hbm,
    conv_ref,
    own_hbm,
    other_hbm,
    vectors_ref,
    out_hbm,
    *refs,
):
    sent_hbm, grad_conv_ref = refs[:block_frames], refs[block_frames]
    (
        frames_ref,
        lifted_ref,
        cotangent_ref,
        own_ref,
        other_ref,
        out_ref,
        sent_ref,
        in_sems,
        out_sems,
    ) = refs[block_frames + 1 :]
    tokens, features = frames_ref.shape
    half = features // cores
    share, half_blocks = sent_ref.shape[-1], sent_ref.shape[2] // cores
    core, place = index_ref[0], index_ref[1]
    conv = conv_ref[...]
    def columns(start, side):
        return pl.ds(pl.multiple_of(side * half + start, lanes), chunk)

    pieces, loads = [], []
    for weight_hbm, weight_ref, side in (
        (other_hbm, other_ref, 1 - core),
        (own_hbm, own_ref, core),
    ):
        for start in range(0, half, chunk):
            where, rows, slot = columns(start, side), pl.ds(start, chunk), 2 * len(pieces)
            pieces.append((weight_ref, start, side))
            pair = (
                pltpu.make_async_copy(
                    weight_hbm.at[rows, :], weight_ref.at[rows, :], in_sems.at[slot]
                ),
                pltpu.make_async_copy(
                    frames_hbm.at[:, where], frames_ref.at[:, where], in_sems.at[slot + 1]
                ),
            )
            loads.append(pair)
            for copy in pair:
                copy.start()
    load = pltpu.make_async_copy(cotangent_hbm, cotangent_ref, in_sems.at[2 * len(pieces)])
    load.start()

    total = jnp.zeros((tokens, lanes), wide)
    for number, (weight_ref, start, side) in enumerate(pieces):
        for copy in loads[number]:
            copy.wait()
        where = columns(start, side)
        raised = outer_rows(conv, weight_ref[start : start + chunk, :])
        lifted = (frames_ref[:, where].astype(wide) + raised + vectors_ref[0:1, where]).astype(narrow)
        lifted_ref[:, where] = lifted
        total = total + folded(lifted.astype(wide))
    center = jnp.sum(total, axis=1, keepdims=True) / features

    load.wait()
    squares = jnp.zeros((tokens, lanes), wide)
    plain = jnp.zeros((tokens, lanes), wide)
    crossed = jnp.zeros((tokens, lanes), wide)
    for weight_ref, start, side in pieces:
        where = columns(start, side)
        shifted = lifted_ref[:, where].astype(wide) - center
        scaled = cotangent_ref[:, where].astype(wide) * vectors_ref[1:2, where]
        squares = squares + folded(shifted * shifted)
        plain = plain + folded(scaled)
        crossed = crossed + folded(scaled * shifted)
    inverse = lax.rsqrt(jnp.sum(squares, axis=1, keepdims=True) / features + epsilon)
    mean_plain = jnp.sum(plain, axis=1, keepdims=True) / features
    mean_crossed = inverse * jnp.sum(crossed, axis=1, keepdims=True) / features

    grad_conv = jnp.zeros(grad_conv_ref.shape, wide)
    stores = []
    for number, (weight_ref, start, side) in enumerate(pieces):
        where = columns(start, side)
        unit = (lifted_ref[:, where].astype(wide) - center) * inverse
        gain = vectors_ref[1:2, where]
        out_ref[:, where] = (unit * gain).astype(narrow)
        stores.append(
            pltpu.make_async_copy(
                out_ref.at[:, where], out_hbm.at[:, where], out_sems.at[block_frames + number]
            )
        )
        stores[-1].start()
        scaled = cotangent_ref[:, where].astype(wide) * gain
        grad = (inverse * (scaled - mean_plain - unit * mean_crossed)).astype(narrow)
        for piece in range(chunk // share):
            slot = start // share + piece
            member, block = slot % members // cores, side * half_blocks + slot // members
            sent_ref[place ^ member, core ^ (slot % cores), block] = grad[
                :, piece * share : (piece + 1) * share
            ]
        grad_conv = grad_conv + jnp.dot(
            grad, weight_ref[start : start + chunk, :], preferred_element_type=wide
        )
    for step in range(block_frames):
        stores.append(
            pltpu.make_async_copy(sent_ref.at[step], sent_hbm[step], out_sems.at[step])
        )
        stores[-1].start()
    grad_conv_ref[...] = grad_conv.astype(narrow)
    for copy in stores:
        copy.wait()


def lift(index, frames_in, cotangent, conv, own, other, bias, gain, blocks, share):
    tokens, features = frames_in.shape
    channels = conv.shape[1]
    vmem = pl.BlockSpec(memory_space=pltpu.VMEM)
    hbm = pl.BlockSpec(memory_space=pltpu.HBM)
    return pl.pallas_call(
        lift_kernel,
        out_shape=(
            jax.ShapeDtypeStruct((tokens, features), narrow),
            *[jax.ShapeDtypeStruct((cores, blocks, tokens, share), narrow)] * block_frames,
            jax.ShapeDtypeStruct((tokens, channels), narrow),
        ),
        in_specs=[pl.BlockSpec(memory_space=pltpu.SMEM), hbm, hbm, vmem, hbm, hbm, vmem],
        out_specs=(hbm,) * (1 + block_frames) + (vmem,),
        scratch_shapes=[
            pltpu.VMEM((tokens, features), narrow),
            pltpu.VMEM((tokens, features), narrow),
            pltpu.VMEM((tokens, features), narrow),
            pltpu.VMEM(own.shape, narrow),
            pltpu.VMEM(own.shape, narrow),
            pltpu.VMEM((tokens, features), narrow),
            pltpu.VMEM((block_frames, cores, blocks, tokens, share), narrow),
            pltpu.SemaphoreType.DMA((1 + 2 * (features // chunk),)),
            pltpu.SemaphoreType.DMA((block_frames + features // chunk,)),
        ],
        compiler_params=pltpu.CompilerParams(vmem_limit_bytes=60 * 1024 * 1024),
        cost_estimate=pl.CostEstimate(
            flops=0,
            bytes_accessed=0,
            transcendentals=0,
        ),
        name="lift",
    )(index, frames_in, cotangent, conv, own, other, jnp.stack([bias, gain]))


def split_kernel(index_ref, value_ref, *out_refs):
    core, place = index_ref[0], index_ref[1]
    blocks, share = out_refs[0].shape[1], out_refs[0].shape[-1]
    for member in range(block_frames):
        for step in range(block_frames):

            @pl.when((place ^ step) == member)
            def _():
                for block in range(blocks):
                    for side in range(cores):
                        start = ((block * block_frames + member) * cores + side) * share
                        out_refs[step][core ^ side, block] = value_ref[:, start : start + share]


def split(index, value, blocks, share):
    vmem = pl.BlockSpec(memory_space=pltpu.VMEM)
    part = jax.ShapeDtypeStruct((cores, blocks, value.shape[0], share), value.dtype)
    return pl.pallas_call(
        split_kernel,
        out_shape=(part,) * block_frames,
        in_specs=[pl.BlockSpec(memory_space=pltpu.SMEM), vmem],
        out_specs=(vmem,) * block_frames,
        compiler_params=pltpu.CompilerParams(vmem_limit_bytes=16 * 1024 * 1024),
        name="split",
    )(index, value)


def squeeze_kernel(index_ref, frames_ref, weight_ref, start_ref, out_ref, *, side):
    half = weight_ref.shape[0]
    columns = pl.ds(pl.multiple_of((index_ref[0] ^ side) * half, lanes), half)
    total = start_ref[...] + jnp.dot(
        frames_ref[:, columns], weight_ref[...], preferred_element_type=wide
    )
    out_ref[...] = total.astype(out_ref.dtype)


def squeeze(index, frames_in, weight, start, side, dtype):
    vmem = pl.BlockSpec(memory_space=pltpu.VMEM)
    return pl.pallas_call(
        functools.partial(squeeze_kernel, side=side),
        out_shape=jax.ShapeDtypeStruct((frames_in.shape[0], weight.shape[1]), dtype),
        in_specs=[pl.BlockSpec(memory_space=pltpu.SMEM)] + [vmem] * 3,
        out_specs=vmem,
        compiler_params=pltpu.CompilerParams(vmem_limit_bytes=24 * 1024 * 1024),
        name="squeeze",
    )(index, frames_in, weight, start)


def block_frames_of(index_ref, refs):
    place, has_low, has_high = [index_ref[k] for k in range(3)]
    odd, upper = place % 2 == 1, place // 2 == 1
    parts = [ref[...].astype(wide) for ref in refs]
    low = [jnp.where(odd, parts[j ^ 1], parts[j]) for j in range(block_frames)]
    full = [jnp.where(upper, low[j ^ 2], low[j]) for j in range(block_frames)]
    before = jnp.where(has_low > 0, parts[block_frames], 0.0)
    behind = jnp.where(has_high > 0, parts[block_frames + 1], 0.0)
    return [before] + full + [behind]


def mix_grad_kernel(index_ref, taps_ref, *refs):
    earlier, same, later = [taps_ref[k : k + 1, :] for k in range(3)]
    per_core = block_frames + 2
    for side in range(cores):
        grads = block_frames_of(index_ref, refs[side * per_core : (side + 1) * per_core])
        for f in range(block_frames):
            mixed = earlier * grads[f + 2] + same * grads[f + 1] + later * grads[f]
            refs[-1][side, f ^ index_ref[0]] = mixed.astype(narrow)


def mix_conv_kernel(index_ref, taps_ref, grad_ref, *refs):
    earlier, same, later = [taps_ref[k : k + 1, :] for k in range(3)]
    per_core = block_frames + 2
    *inputs, conv_ref, small_ref = refs
    sums = [0.0] * 4
    for side in range(cores):
        bottles = block_frames_of(index_ref, inputs[side * per_core : (side + 1) * per_core])
        grads = inputs[cores * per_core + side * block_frames :][:block_frames]
        for f in range(block_frames):
            down, here, up = bottles[f : f + 3]
            conv_ref[side, f ^ index_ref[0]] = (
                earlier * down + same * here + later * up
            ).astype(narrow)
        for step in range(block_frames):
            grad = grads[step][...].astype(wide)
            f = index_ref[0] ^ step
            mixed = grad_ref[side, step].astype(wide)
            near = [
                sum(jnp.where(f == j, bottles[j + k], 0.0) for j in range(block_frames))
                for k in range(3)
            ]
            for k, value in enumerate([v * grad for v in near] + [mixed]):
                sums[k] = sums[k] + jnp.sum(value, axis=0, keepdims=True)
    small_ref[...] = jnp.zeros_like(small_ref)
    for k in range(4):
        small_ref[k : k + 1, :] = sums[k]


def mix(index, taps, parts, grad_rows=None):
    tokens, channels = parts[0].shape
    vmem = pl.BlockSpec(memory_space=pltpu.VMEM)
    rows = jax.ShapeDtypeStruct((cores, block_frames, tokens, channels), narrow)
    last = grad_rows is None
    operands = list(parts) if last else [grad_rows, *parts]
    return pl.pallas_call(
        mix_grad_kernel if last else mix_conv_kernel,
        out_shape=rows if last else (rows, jax.ShapeDtypeStruct((8, channels), wide)),
        in_specs=[pl.BlockSpec(memory_space=pltpu.SMEM)] + [vmem] * (1 + len(operands)),
        out_specs=vmem if last else (vmem, vmem),
        compiler_params=pltpu.CompilerParams(vmem_limit_bytes=24 * 1024 * 1024),
        name="mix_grad" if last else "mix_conv",
    )(index, taps, *operands)


def contract_kernel(targets_ref, rows_ref, small_ref, *refs):
    own, other = refs[:block_frames], refs[block_frames:members]
    total_ref, bias_ref, *sent_refs = refs[members:-1]
    extra_ref = refs[-1]
    share, channels = total_ref.shape

    def product(target):
        total = jnp.zeros((share, channels), wide)
        bias = jnp.zeros((1, share), wide)
        for step in range(block_frames):
            for side, value in ((0, own[step][0, target]), (1, other[step][target])):
                total = total + inner_rows(value, rows_ref[side, step])
                bias = bias + jnp.sum(value.astype(wide), axis=0, keepdims=True)
        return total, bias

    for index, sent_ref in enumerate(sent_refs):
        total, bias = product(targets_ref[index + 1])
        sent_ref[:share, :] = total.astype(narrow)
        if small_ref is not None:
            extra_ref[...] = jnp.zeros_like(extra_ref)
            extra_ref[0:4, :] = small_ref[0:4, :]
            extra_ref[4:5, :share] = bias
            high = extra_ref[0:8, :].astype(narrow).astype(wide)
            extra_ref[8:16, :] = extra_ref[0:8, :] - high
            sent_ref[share:, :] = extra_ref[...].astype(narrow)
    total_ref[...], bias_ref[...] = product(targets_ref[0])


def contract(targets, rows, small, parts):
    share, channels = parts[0].shape[-1], rows.shape[-1]
    blocks = parts[0].shape[1]
    vmem = pl.BlockSpec(memory_space=pltpu.VMEM)
    body = contract_kernel
    operands = [targets, rows] + ([] if small is None else [small]) + list(parts)
    if small is None:
        body = lambda targets_ref, rows_ref, *refs: contract_kernel(
            targets_ref, rows_ref, None, *refs
        )
    sent = jax.ShapeDtypeStruct((share + (0 if small is None else 16), channels), narrow)
    return pl.pallas_call(
        body,
        out_shape=(
            jax.ShapeDtypeStruct((share, channels), wide),
            jax.ShapeDtypeStruct((1, share), wide),
        )
        + (sent,) * (blocks - 1),
        in_specs=[pl.BlockSpec(memory_space=pltpu.SMEM)] + [vmem] * (len(operands) - 1),
        out_specs=(vmem,) * (blocks + 1),
        scratch_shapes=[pltpu.VMEM((16, channels), wide)],
        compiler_params=pltpu.CompilerParams(vmem_limit_bytes=24 * 1024 * 1024),
        name="contract_down" if small is None else "contract_up",
    )(*operands)


def after(values, other):
    return list(lax.optimization_barrier((tuple(values), other))[0])


def local(frames_in, cotangent, down_weight, down_bias, conv_kernel, up_weight, up_bias, ln_gain):
    tokens, features = frames_in.shape
    channels = down_weight.shape[1]
    count = lax.axis_size("tm")
    blocks = count // block_frames
    share = features // (count * cores)
    frame, core = lax.axis_index("tm"), lax.axis_index("tensor")
    block, place = frame // block_frames, frame % block_frames
    groups = [
        list(range(start, start + members)) for start in range(0, count * cores, members)
    ]

    def core_swap(value):
        return lax.ppermute(value, "tensor", [(0, 1), (1, 0)])

    def block_swap(value, step):
        return lax.ppermute(value, "tm", [(i, i ^ step) for i in range(count)])

    def to_members(value):
        return lax.all_to_all(
            value,
            ("tm", "tensor"),
            split_axis=0,
            concat_axis=0,
            tiled=True,
            axis_index_groups=groups,
        )

    def edge_swap(value):
        edges = range(block_frames - 1, count - 1, block_frames)
        return lax.ppermute(
            value, "tm", [p for i in edges for p in ((i, i + 1), (i + 1, i))]
        )

    def across(value, step):
        return lax.ppermute(
            value, "tm", [(i, (i + step * block_frames) % count) for i in range(count)]
        )

    def shifted(value, step):
        pairs = [(i, i + step * block_frames) for i in range(count)]
        return lax.ppermute(value, "tm", [p for p in pairs if 0 <= p[1] < count])

    def ordered(parts):
        low = [
            jnp.where(place % 2 == 1, parts[j ^ 1], parts[j]) for j in range(block_frames)
        ]
        return [jnp.where(place // 2 == 1, low[j ^ 2], low[j]) for j in range(block_frames)]

    index = jnp.stack([core, place]).astype(jnp.int32)
    down_other = core_swap(down_weight)
    frames_parts = list(
        split(index, frames_in, blocks, share)
    )
    index_after = after([index], frames_parts[3])[0]
    for step in (1, 2):
        frames_parts[step] = block_swap(frames_parts[step], step)
    bottle = squeeze(index_after, frames_in, down_weight, down_bias[None], 0, wide)
    bottle = squeeze(index, frames_in, down_other, bottle, 1, narrow)
    bottle = after([bottle], frames_parts[1:3])[0]
    up_other = core_swap(up_weight)
    bottle_edge = edge_swap(bottle)
    bottle_parts = [
        bottle,
        block_swap(bottle, 1),
        block_swap(after([bottle], bottle_edge)[0], 2),
        block_swap(bottle, 3),
    ]
    frames_parts[3] = block_swap(
        after([frames_parts[3]], (bottle_parts[1], bottle_parts[3], bottle_edge))[0], 3
    )

    def pick(value, *places):
        chosen = sum([(place == p) for p in places[1:]], place == places[0])
        return jnp.where(chosen, value, 0.0)

    earlier, same, later = conv_kernel
    odd = place % 2 == 1
    conv = (
        jnp.where(odd, earlier, later) * bottle_parts[1].astype(wide)
        + same * bottle.astype(wide)
        + (pick(later, 1) + pick(earlier, 2)) * bottle_parts[3].astype(wide)
        + (pick(earlier, 0) + pick(later, 3)) * bottle_edge.astype(wide)
    ).astype(narrow)
    out_tokens, *grad_sent, grad_conv = lift(
        index,
        frames_in,
        cotangent,
        conv,
        up_weight,
        up_other,
        up_bias,
        ln_gain,
        blocks,
        share,
    )
    grad_conv, *grad_sent = after([grad_conv, *grad_sent], frames_parts[1:])
    grad_parts = [grad_conv] + [block_swap(grad_conv, step) for step in range(1, block_frames)]
    grad_sent = after(grad_sent, grad_parts[1])
    lifted_parts = [grad_sent[0]] + [
        block_swap(grad_sent[step], step) for step in range(1, block_frames)
    ]

    def by_core(parts):
        return list(parts) + [core_swap(v[1]) for v in parts]

    frames_got = by_core(after(frames_parts, grad_parts[1]))

    def whole_block(parts, late):
        if blocks == 2:
            beside = across(
                lax.select_n(jnp.where(block == 0, block_frames - 1, 0) ^ place, *parts), 1
            )
            sides = [beside, beside]
        else:
            frames = ordered(parts)
            sides = [shifted(frames[-1], 1), shifted(frames[0], -1)]
        if late is not None:
            sides = after(sides, late)
        own = list(parts) + sides[: 1 if blocks == 2 else 2]
        other = [core_swap(value) for value in own]
        return own[:block_frames] + sides, other[:block_frames] + [other[block_frames], other[-1]]

    grad_own, grad_other = whole_block(grad_parts, None)
    ends = jnp.stack([place, block, blocks - 1 - block]).astype(jnp.int32)
    grad_bottle = mix(ends, conv_kernel, after(grad_own + grad_other, lifted_parts[1:3]))
    targets = jnp.stack([(block + step) % blocks for step in range(blocks)]).astype(jnp.int32)
    grad_down, _, *down_sent = contract(targets, grad_bottle, None, frames_got)
    bottle_own, bottle_other = whole_block(
        after(bottle_parts, grad_parts[3]), lifted_parts[2]
    )
    conv_rows, small = mix(
        ends,
        conv_kernel,
        bottle_own + bottle_other + grad_own[:block_frames] + grad_other[:block_frames],
        grad_bottle,
    )
    down_got = [across(value, step + 1) for step, value in enumerate(down_sent)]
    grad_up, grad_up_bias, *up_sent = contract(targets, conv_rows, small, by_core(lifted_parts))
    up_got = [across(value, step + 1) for step, value in enumerate(up_sent)]
    down_got = after(down_got, up_sent[0])
    grad_up_bias, small = grad_up_bias[0], small[:5]
    small = small.at[4, :share].set(grad_up_bias)
    for down, up in zip(down_got, up_got):
        down, up = down.astype(wide), up.astype(wide)
        grad_down = grad_down + down[:share]
        grad_up = grad_up + up[:share]
        small = small + up[share : share + 5] + up[share + 8 : share + 13]
    grad_up_bias = small[4, :share]
    return (out_tokens, grad_down, grad_up, grad_up_bias, small[3], small[:3])


def solution(mesh):
    tokens = P(("groups", "tm", "tensor"), None)
    return jax.shard_map(
        local,
        mesh=mesh,
        in_specs=(tokens, tokens, P("tensor", None), P(), P(), P("tensor", None), P(), P()),
        out_specs=(
            tokens,
            tokens,
            tokens,
            P(("groups", "tm", "tensor")),
            P("groups"),
            P("groups", None),
        ),
        check_vma=False,
    )
```
